512 devices in a mesh: lat: 16 (over x, y_lo, core), lon: 32 (over z, y_hi).
Axes of the slice: x: 4, y: 8 (y_hi: 4, y_lo: 2; y = y_hi * 2 + y_lo), z: 8, core: 2. Of those that a mesh axis runs over, the one named last changes fastest.
Arguments:
- queries: bfloat16 [256, 512, 512], P('lat', 'lon'), may hold values from -12 to 12
- keys: bfloat16 [256, 512, 512], P('lat', 'lon'), may hold values from -12 to 12
- values: bfloat16 [256, 512, 512], P('lat', 'lon'), may hold values from -6 to 6
- out_grad: bfloat16 [256, 512, 512], P('lat', 'lon'), may hold values from -16 to 16
- pos_bias: float32 [8, 13, 13], replicated, may hold values from -0.5 to 0.5
Outputs:
- q_grad: bfloat16 [256, 512, 512], P('lat', 'lon')
- k_grad: bfloat16 [256, 512, 512], P('lat', 'lon')
- v_grad: bfloat16 [256, 512, 512], P('lat', 'lon')
The draws below stay inside these ranges and needn't reach their ends.
All inputs are finite; a program needn't handle non-finite values.
Results may differ from the reference program's by a relative error of at most 0.006.
Values may be sent and summed in bfloat16 or wider, within the bound.
A program may use at most 64 MiB of HBM per device.

```python
import jax
import jax.numpy as jnp
from jax import lax

D = 512
HEADS = 8
WINDOW = 13
HEAD_DIM = 64
RADIUS = 6
NLAT = 256
NLON = 512


def drawn_field(key, salt):
    field_key = jax.random.fold_in(key, salt)
    return jax.random.truncated_normal(field_key, -6.0, 6.0, (NLAT, NLON, D), jnp.float32)


def draw_queries(key, part):
    field = drawn_field(key, 1)
    return field.astype(jnp.bfloat16)


def draw_keys(key, part):
    field = drawn_field(key, 2)
    return field.astype(jnp.bfloat16)


def block_scale(key, extent, shards, least, largest):
    def one(position, parts):
        draws = jax.random.uniform(jax.random.fold_in(jax.random.fold_in(key, 6), position), (parts,), jnp.float32, least / len(shards), largest / len(shards))
        return jnp.repeat(jnp.exp(draws), extent[position] // parts).reshape((-1,) + (1,) * (len(extent) - position - 1))

    factor_of = one(*shards[0])
    for cut in shards[1:]:
        factor_of = factor_of * one(*cut)
    return factor_of


def scatter_about(rng, dims, width, reach, cuts=(), kind=jnp.bfloat16):
    factor_of = block_scale(rng, dims, cuts, -0.22, 0.18) if cuts else 1.0
    values = jax.random.normal(rng, dims, jnp.float32) * width * factor_of
    return jnp.minimum(jnp.maximum(values, -reach), reach).astype(kind)


def setup_inputs(seed: int = 0) -> dict:
    streams_of = jax.random.split(jax.random.key(seed), 6)
    queries = draw_queries(jax.random.fold_in(streams_of[5], 71), 0)
    keys = draw_keys(jax.random.fold_in(streams_of[5], 71), 0)
    values = scatter_about(streams_of[2], (NLAT, NLON, D), 1.0, 6.0, ((0, 16), (1, 32)))
    out_grad = scatter_about(streams_of[3], (NLAT, NLON, D), 4.0, 16.0, ((0, 16), (1, 32)))
    pos_bias = jnp.clip(jax.random.uniform(streams_of[4], (HEADS, WINDOW, WINDOW), jnp.float32, -0.5, 0.5), -0.5, 0.5)
    return dict(queries=queries, keys=keys, values=values, out_grad=out_grad, pos_bias=pos_bias)


def pad_grid(field):
    wrapped = jnp.concatenate([field[:, NLON - RADIUS:], field, field[:, :RADIUS]], axis=1)
    border = jnp.zeros((RADIUS,) + wrapped.shape[1:], wrapped.dtype)
    return jnp.concatenate([border, wrapped, border], axis=0)


def windows(padded, row_index, flipped):
    band_rows = lax.dynamic_slice_in_dim(padded, row_index, WINDOW, 0)
    if flipped:
        band_rows = band_rows[::-1]
        slice_starts = [WINDOW - 1 - offset_index for offset_index in range(WINDOW)]
    else:
        slice_starts = list(range(WINDOW))
    return jnp.stack([band_rows[:, slice_start:slice_start + NLON] for slice_start in slice_starts], axis=1)


def split_heads(block):
    return block.reshape(block.shape[:-1] + (HEADS, HEAD_DIM)).astype(jnp.float32)


def rounded(field):
    return lax.optimization_barrier(field.astype(jnp.bfloat16)).astype(jnp.float32)


def reference(queries, keys, values, out_grad, pos_bias):
    score_scale = HEAD_DIM ** -0.5
    offset_rows = jnp.arange(WINDOW, dtype=jnp.int32) - RADIUS
    key_pad = pad_grid(keys)
    value_pad = pad_grid(values)

    def query_row(row_index):
        query_heads = split_heads(lax.dynamic_index_in_dim(queries, row_index, 0, keepdims=False))
        grad_heads = split_heads(lax.dynamic_index_in_dim(out_grad, row_index, 0, keepdims=False))
        key_win = split_heads(windows(key_pad, row_index, False))
        value_win = split_heads(windows(value_pad, row_index, False))
        scores = jnp.einsum('xhd,abxhd->xhab', query_heads, key_win) * score_scale + pos_bias[None]
        key_rows = row_index + offset_rows
        valid = ((key_rows >= 0) & (key_rows < NLAT))[None, None, :, None]
        scores = jnp.where(valid, scores, -jnp.inf)
        row_top = jnp.max(scores, axis=(2, 3), keepdims=True)
        log_total = row_top + jnp.log(jnp.sum(jnp.exp(scores - row_top), axis=(2, 3), keepdims=True))
        probability = jnp.exp(scores - log_total)
        prob_grad = jnp.einsum('xhd,abxhd->xhab', grad_heads, value_win)
        row_delta = jnp.sum(probability * prob_grad, axis=(2, 3), keepdims=True)
        score_grad = rounded(probability * (prob_grad - row_delta))
        query_grad = score_scale * jnp.einsum('xhab,abxhd->xhd', score_grad, key_win)
        return query_grad.reshape(NLON, D).astype(jnp.bfloat16), log_total[:, :, 0, 0], row_delta[:, :, 0, 0]

    all_rows = jnp.arange(NLAT, dtype=jnp.int32)
    q_grad, log_totals, deltas = lax.map(query_row, all_rows)

    query_pad = pad_grid(queries)
    grad_pad = pad_grid(out_grad)
    total_pad = pad_grid(log_totals)
    delta_pad = pad_grid(deltas)

    def key_row(row_index):
        key_heads = split_heads(lax.dynamic_index_in_dim(keys, row_index, 0, keepdims=False))
        value_heads = split_heads(lax.dynamic_index_in_dim(values, row_index, 0, keepdims=False))
        query_win = split_heads(windows(query_pad, row_index, True))
        grad_win = split_heads(windows(grad_pad, row_index, True))
        total_win = jnp.transpose(windows(total_pad, row_index, True), (2, 3, 0, 1))
        delta_win = jnp.transpose(windows(delta_pad, row_index, True), (2, 3, 0, 1))
        scores = jnp.einsum('abxhd,xhd->xhab', query_win, key_heads) * score_scale + pos_bias[None]
        query_rows = row_index + RADIUS - jnp.arange(WINDOW, dtype=jnp.int32)
        valid = ((query_rows >= 0) & (query_rows < NLAT))[None, None, :, None]
        probability = jnp.where(valid, jnp.exp(scores - total_win), 0.0)
        prob_grad = jnp.einsum('abxhd,xhd->xhab', grad_win, value_heads)
        score_grad = rounded(probability * (prob_grad - delta_win))
        prob_low = rounded(probability)
        key_grad = score_scale * jnp.einsum('xhab,abxhd->xhd', score_grad, query_win)
        value_grad = jnp.einsum('xhab,abxhd->xhd', prob_low, grad_win)
        return key_grad.reshape(NLON, D).astype(jnp.bfloat16), value_grad.reshape(NLON, D).astype(jnp.bfloat16)

    k_grad, v_grad = lax.map(key_row, all_rows)
    return (q_grad, k_grad, v_grad)
```

```python
import functools

import jax
import jax.numpy as jnp
from jax import lax
from jax.experimental import pallas as pl
from jax.experimental.pallas import tpu as pltpu
from jax.sharding import PartitionSpec as P

WINDOW = 13
RADIUS = 6
HEADS = 8
HEAD_DIM = 64
ROWS = 16
COLS = 16
KEY_ROWS = ROWS + 2 * RADIUS
WIDE = 32
BAND = 4
BANDS = ROWS // BAND
DEEP = BAND + 2 * RADIUS
WIDTH = HEADS * HEAD_DIM
OWN = BAND * COLS
NEAR = DEEP * COLS
TOKENS = ROWS * COLS
EDGE = ROWS * RADIUS
RIM = RADIUS * COLS
GROUP = 4
PARTS = HEADS // GROUP
GW = GROUP * HEAD_DIM
QL = GROUP * OWN
EDGE_LANES = GROUP * BAND * RADIUS
STRIP = 384
NEG = -1e30
MESH = pl.DeviceIdType.MESH
F32 = jnp.float32
BF16 = jnp.bfloat16


def iota(shape, dim):
    return lax.broadcasted_iota(jnp.int32, shape, dim)


def sixth(j):
    return lax.shift_right_logical(j * 10923, 16)


def sel(mask):
    return jnp.where(mask, 1.0, 0.0).astype(BF16)


def onehot(rows, cols, target):
    return sel(target == iota((rows, cols), 1))


def dot(a, b):
    return jnp.dot(a, b, preferred_element_type=F32)


def dot_t(a, b):
    return lax.dot_general(a, b, (((1,), (1,)), ((), ())), preferred_element_type=F32)


def t_dot(a, b):
    return lax.dot_general(a, b, (((0,), (0,)), ((), ())), preferred_element_type=F32)


def dot3(a, pick):
    hi = a.astype(BF16)
    rest = a - hi.astype(F32)
    mid = rest.astype(BF16)
    low = (rest - mid.astype(F32)).astype(BF16)
    return dot(hi, pick) + dot(mid, pick) + dot(low, pick)


def edge_token(j, start):
    r = sixth(j)
    return r * COLS + (j - r * RADIUS) + start


def edge_index(token, west, east):
    r = lax.shift_right_logical(token, 4)
    c = lax.bitwise_and(token, 15)
    at = r * RADIUS + c
    in_west = (c >= west) & (c < west + RADIUS)
    in_east = (c >= east) & (c < east + RADIUS)
    return jnp.where(in_west, at - west, jnp.where(in_east, at - east + EDGE, -1))


def pick_lanes(start):
    j = iota((QL, 128), 1)
    return sel((iota((QL, 128), 0) == edge_token(j, start)) & (j < EDGE_LANES))


def put_lanes(start):
    j = iota((128, QL), 0)
    return sel((iota((128, QL), 1) == edge_token(j, start)) & (j < EDGE_LANES))


def combine(a, b, shared):
    m0 = a[0:BANDS]
    m1 = jnp.where(shared, b[0:BANDS], NEG)
    m = jnp.maximum(m0, m1)
    w0 = jnp.exp(m0 - m)
    w1 = jnp.exp(m1 - m)
    total = a[BANDS:2 * BANDS] * w0 + b[BANDS:2 * BANDS] * w1
    weighed = a[2 * BANDS:] * w0 + b[2 * BANDS:] * w1
    return m + jnp.log(total), weighed / total


def kernel(nlat, nlon, q_ref, k_ref, v_ref, g_ref, bias_ref, dq_ref, dk_ref, dv_ref,
           qg, kv, send, land, table, scores, dprobs, srow, final,
           psend, pland, osend, oland, own_dq, halo_dq, dsend, dland, acc, lsend, lland,
           biases, bias, ss, rs, ins):
    lat = lax.axis_index("lat")
    lon = lax.axis_index("lon")
    east = (lat, lax.rem(lon + 1, nlon))
    west = (lat, lax.rem(lon + nlon - 1, nlon))
    north = (lat - 1, lon)
    south = (lat + 1, lon)
    has_north = lat > 0
    has_south = lat < nlat - 1

    loads = [pltpu.make_async_copy(ref, dst, ins.at[i]) for i, (ref, dst) in enumerate((
        (q_ref, qg.at[0, pl.ds(0, ROWS), pl.ds(0, COLS)]),
        (g_ref, qg.at[1, pl.ds(0, ROWS), pl.ds(0, COLS)]),
        (k_ref, kv.at[0, pl.ds(RADIUS, ROWS)]),
        (v_ref, kv.at[1, pl.ds(RADIUS, ROWS)]),
        (bias_ref, bias)))]
    for c in loads:
        c.start()

    bar = pltpu.get_barrier_semaphore()
    pl.semaphore_signal(bar, 1, device_id=east, device_id_type=MESH)
    pl.semaphore_signal(bar, 1, device_id=west, device_id_type=MESH)

    @pl.when(has_north)
    def _():
        pl.semaphore_signal(bar, 1, device_id=north, device_id_type=MESH)

    @pl.when(has_south)
    def _():
        pl.semaphore_signal(bar, 1, device_id=south, device_id_type=MESH)

    def lanes(g):
        return slice(g * GW, (g + 1) * GW)

    def pack_edges(dst, t, tokens, starts):
        for d in range(2):
            pick = onehot(EDGE, TOKENS, edge_token(iota((EDGE, TOKENS), 0), starts[d]))
            got = dot(pick, tokens).astype(BF16)
            for g in range(PARTS):
                dst[g, t, d] = got[:, lanes(g)]

    for t in range(2):
        loads[t].wait()
        tokens = qg[t, :, 0:COLS, :].reshape(TOKENS, WIDTH)
        pack_edges(send, t, tokens, (COLS - RADIUS, 0))
    for c in loads[2:]:
        c.wait()
    peers = 2 + has_north.astype(jnp.int32) + has_south.astype(jnp.int32)
    pl.semaphore_wait(bar, peers)

    along = (east, west)
    across = (south, north)

    def remote(g, i, src, dst, to):
        return pltpu.make_async_remote_copy(
            src, dst, ss.at[g, i], rs.at[g, i], device_id=to, device_id_type=MESH)

    def lon_copy(g, t, d):
        return remote(g, 2 * t + d, send.at[g, t, d], land.at[g, t, d], along[d])

    def kv_mid(g):
        span = pl.ds(g * GW, GW)
        return lambda d: [remote(
            g, 4 + 2 * t + d,
            kv.at[t, pl.ds(ROWS if d == 0 else RADIUS, RADIUS), pl.ds(0, COLS), span],
            kv.at[t, pl.ds(0 if d == 0 else ROWS + RADIUS, RADIUS), pl.ds(0, COLS), span],
            across[d]) for t in range(2)]

    def own_copy(g, d):
        return remote(g, 8 + d, osend.at[g, d], oland.at[g, d], along[d])

    def part_copy(g, d):
        return remote(g, 10 + d, psend.at[g, d], pland.at[g, d], along[d])

    def dq_copy(g, d):
        return remote(g, 12 + d, dsend.at[g, 0, d], dland.at[g, d], along[d])

    def lat_back(g):
        return lambda d: [remote(g, 14 + d, lsend.at[g, d], lland.at[g, d], across[d])]

    out_ok = (has_south, has_north)
    in_ok = (has_north, has_south)

    def lat_do(make, ok, what):
        for d in range(2):
            @pl.when(ok[d])
            def _(d=d):
                for c in make(d):
                    what(c)

    def start_lat(make):
        lat_do(make, out_ok, lambda c: c.start())

    def recv_lat(make):
        lat_do(make, in_ok, lambda c: c.wait_recv())

    def sent_lat(make):
        lat_do(make, out_ok, lambda c: c.wait_send())

    def start_lon(g):
        for t in range(2):
            for d in range(2):
                lon_copy(g, t, d).start()

    start_lat(kv_mid(0))
    start_lat(kv_mid(1))
    start_lon(0)
    start_lon(1)

    @pl.when(jnp.logical_not(has_north))
    def _():
        kv[:, 0:RADIUS] = jnp.zeros((2, RADIUS, COLS, WIDTH), BF16)

    @pl.when(jnp.logical_not(has_south))
    def _():
        kv[:, RADIUS + ROWS:KEY_ROWS] = jnp.zeros((2, RADIUS, COLS, WIDTH), BF16)

    acc[...] = jnp.zeros((2, KEY_ROWS * COLS, WIDTH), F32)

    biases[...] = jnp.zeros((128, 128), F32)
    for a in range(WINDOW):
        biases[a * HEADS:(a + 1) * HEADS, 0:WINDOW] = bias[a]
    turned = jnp.transpose(biases[...])[0:16, :]
    row = iota((128, STRIP), 0)
    step = 15 - lax.shift_right_logical(iota((128, STRIP), 1), 4)
    w = lax.shift_right_logical(iota((COLS, STRIP), 1), 4)
    cc = lax.bitwise_and(iota((COLS, STRIP), 1), 15)
    in_window = (w >= 3) & (w < 3 + WINDOW)
    key_col = iota((COLS, STRIP), 0) + RADIUS
    halo_col = jnp.where(cc < RADIUS, cc - RADIUS, cc + COLS - RADIUS)
    offsets = (jnp.where(in_window, key_col - cc, -1),
               jnp.where(in_window & (cc < 2 * RADIUS), key_col - halo_col, -1))
    for h in range(HEADS):
        spread = dot3(turned, sel(row == step * HEADS + h))
        for half in range(2):
            strip = jnp.full((COLS, STRIP), NEG, F32)
            for b in range(WINDOW):
                strip = jnp.where(offsets[half] == b, spread[b:b + 1, :], strip)
            for r in range(DEEP):
                shift = (DEEP - 1 - r) * COLS
                moved = pltpu.roll(strip, STRIP - shift, 1) if shift else strip
                table[half, r * COLS:(r + 1) * COLS, h * OWN:(h + 1) * OWN] = moved[:, :OWN]

    head_of = lax.shift_right_logical(iota((1, GW), 1), 6)
    keep = [jnp.where(head_of == hh, 1.0, 0.0) for hh in range(GROUP)]
    keep_low = [m.astype(BF16) for m in keep]
    scale = HEAD_DIM ** -0.5

    def stack(x):
        return jnp.concatenate([x * m for m in keep_low], axis=0)

    def unstack(y):
        total = y[0:OWN] * keep[0]
        for hh in range(1, GROUP):
            total = total + y[hh * OWN:(hh + 1) * OWN] * keep[hh]
        return total

    def operands(half, g, lo):
        cols = pl.ds(half * COLS, COLS)
        qt = qg[0, pl.ds(lo, BAND), cols, lanes(g)].reshape(OWN, GW) * scale
        gt = qg[1, pl.ds(lo, BAND), cols, lanes(g)].reshape(OWN, GW)
        kt = kv[0, pl.ds(lo, DEEP), :, lanes(g)].reshape(NEAR, GW)
        return stack(qt.astype(BF16)), stack(gt), kt

    hide_north = jnp.where(has_north, 0.0, NEG)
    hide_south = jnp.where(has_south, 0.0, NEG)

    def score(half, g):
        def body(band):
            lo = band * BAND
            qs, gs, kt = operands(half, g, lo)
            vt = kv[1, pl.ds(lo, DEEP), :, lanes(g)].reshape(NEAR, GW)
            s = dot_t(kt, qs) + table[half, :, g * QL:(g + 1) * QL]
            above = max(RADIUS - lo, 0) * COLS
            below = min(RADIUS + ROWS - lo, DEEP) * COLS
            if above:
                s = jnp.concatenate([s[:above] + hide_north, s[above:]], axis=0)
            if below < NEAR:
                s = jnp.concatenate([s[:below], s[below:] + hide_south], axis=0)
            dp = dot_t(vt, gs)
            scores[half, g * BANDS + band] = s
            dprobs[half, g * BANDS + band] = dp
            m = jnp.max(s, axis=0, keepdims=True)
            e = jnp.exp(s - m)
            srow[half, g, pl.ds(band, 1), :] = m
            srow[half, g, pl.ds(BANDS + band, 1), :] = jnp.sum(e, axis=0, keepdims=True)
            srow[half, g, pl.ds(2 * BANDS + band, 1), :] = jnp.sum(e * dp, axis=0, keepdims=True)

        for band in range(BANDS):
            body(band)
        return srow[half, g, 0:3 * BANDS, :]

    def grad(half, g):
        def body(band):
            lo = band * BAND
            qs, gs, kt = operands(half, g, lo)
            p = jnp.exp(scores[half, g * BANDS + band] - final[half, g, pl.ds(band, 1), :])
            gap = dprobs[half, g * BANDS + band] - final[half, g, pl.ds(BANDS + band, 1), :]
            ds = (p * gap).astype(BF16)
            keys = pl.ds(lo * COLS, NEAR)
            acc[0, keys, lanes(g)] += dot(ds, qs)
            acc[1, keys, lanes(g)] += dot(p.astype(BF16), gs)
            dq = unstack(t_dot(ds, kt)) * scale
            at = pl.ds(band * OWN, OWN)
            if half:
                halo_dq[at, lanes(g)] = dq.astype(BF16)
            else:
                own_dq[at, lanes(g)] = dq

        for band in range(BANDS):
            body(band)

    column = lax.bitwise_and(iota((BANDS, QL), 1), 15)
    spread_lon = onehot(TOKENS, 2 * EDGE, edge_index(iota((TOKENS, 2 * EDGE), 0), 0, RADIUS))
    mine = {}
    parts = {}

    def own_scores(g):
        recv_lat(kv_mid(g))
        mine[g] = score(0, g)
        for d in range(2):
            osend[g, d] = dot3(mine[g], pick_lanes(COLS - RADIUS if d == 0 else 0))
        for d in range(2):
            own_copy(g, d).start()

    def halo_scores(g):
        for t in range(2):
            for d in range(2):
                lon_copy(g, t, d).wait_recv()
            got = dot(spread_lon, land[g, t].reshape(2 * EDGE, GW)).astype(BF16)
            qg[t, :, COLS:WIDE, lanes(g)] = got.reshape(ROWS, 16, GW)
        parts[g] = score(1, g)
        for d in range(2):
            psend[g, d] = dot3(parts[g], pick_lanes(RADIUS if d == 0 else 0))
        for d in range(2):
            part_copy(g, d).start()

    def halo_grads(g):
        theirs = jnp.zeros((3 * BANDS, QL), F32)
        for d in range(2):
            own_copy(g, d).wait_recv()
            theirs = theirs + dot3(oland[g, d], put_lanes(d * RADIUS))
        held = column < 2 * RADIUS
        lse, delta = combine(parts[g], theirs, held)
        final[1, g, 0:BANDS, :] = jnp.where(held, lse, 0.0)
        final[1, g, BANDS:2 * BANDS, :] = jnp.where(held, delta, 0.0)
        grad(1, g)
        for d in range(2):
            start = RADIUS if d == 0 else 0
            pick = onehot(EDGE, TOKENS, edge_token(iota((EDGE, TOKENS), 0), start))
            dsend[g, 0, d] = dot(pick, halo_dq[:, lanes(g)]).astype(BF16)
        for d in range(2):
            dq_copy(g, d).start()

    def own_grads(g):
        theirs = jnp.zeros((3 * BANDS, QL), F32)
        for d in range(2):
            part_copy(g, d).wait_recv()
            theirs = theirs + dot3(pland[g, d], put_lanes(0 if d == 0 else COLS - RADIUS))
        lse, delta = combine(mine[g], theirs, (column < RADIUS) | (column >= COLS - RADIUS))
        final[0, g, 0:BANDS, :] = lse
        final[0, g, BANDS:2 * BANDS, :] = delta
        grad(0, g)
        for t in range(2):
            lsend[g, 0, t] = acc[t, KEY_ROWS * COLS - RIM:, lanes(g)].astype(BF16)
            lsend[g, 1, t] = acc[t, 0:RIM, lanes(g)].astype(BF16)
        start_lat(lat_back(g))

    own_scores(0)
    own_scores(1)
    halo_scores(0)
    halo_scores(1)
    halo_grads(0)
    halo_grads(1)
    own_grads(0)
    own_grads(1)

    spread_dq = onehot(TOKENS, 2 * EDGE,
                       edge_index(iota((TOKENS, 2 * EDGE), 0), 0, COLS - RADIUS))
    for g in range(PARTS):
        for d in range(2):
            dq_copy(g, d).wait_recv()
        dq = own_dq[:, lanes(g)] + dot(spread_dq, dland[g].reshape(2 * EDGE, GW))
        dq_ref[:, :, lanes(g)] = dq.astype(BF16).reshape(ROWS, COLS, GW)
    for g in range(PARTS):
        recv_lat(lat_back(g))
        for t, out in enumerate((dk_ref, dv_ref)):
            first, last = RIM, RIM + TOKENS
            top = acc[t, first:first + RIM, lanes(g)]
            top = top + jnp.where(has_north, lland[g, 0, t].astype(F32), 0.0)
            bottom = acc[t, last - RIM:last, lanes(g)]
            bottom = bottom + jnp.where(has_south, lland[g, 1, t].astype(F32), 0.0)
            middle = acc[t, first + RIM:last - RIM, lanes(g)]
            out[0:RADIUS, :, lanes(g)] = top.astype(BF16).reshape(RADIUS, COLS, GW)
            out[RADIUS:ROWS - RADIUS, :, lanes(g)] = middle.astype(BF16).reshape(
                ROWS - 2 * RADIUS, COLS, GW)
            out[ROWS - RADIUS:ROWS, :, lanes(g)] = bottom.astype(BF16).reshape(RADIUS, COLS, GW)

    for g in range(PARTS):
        for d in range(2):
            for t in range(2):
                lon_copy(g, t, d).wait_send()
            own_copy(g, d).wait_send()
            part_copy(g, d).wait_send()
            dq_copy(g, d).wait_send()
        sent_lat(kv_mid(g))
        sent_lat(lat_back(g))


def hand_on(*refs):
    for i in range(3):
        refs[3 + i][...] = refs[i][...]


def on_device(nlat, nlon, queries, keys, values, out_grad, pos_bias):
    block = jax.ShapeDtypeStruct((ROWS, COLS, WIDTH), BF16)
    vmem = pl.BlockSpec(memory_space=pltpu.VMEM)
    dma = pltpu.SemaphoreType.DMA
    args = (queries, keys, values, out_grad, jnp.transpose(pos_bias, (1, 0, 2)))
    args = [pltpu.with_memory_space_constraint(x, pltpu.HBM) for x in args]
    grads = pl.pallas_call(
        functools.partial(kernel, nlat, nlon),
        out_shape=(block, block, block),
        in_specs=[pl.BlockSpec(memory_space=pltpu.HBM)] * 5,
        out_specs=(vmem,) * 3,
        scratch_shapes=[
            pltpu.VMEM((2, ROWS, WIDE, WIDTH), BF16),
            pltpu.VMEM((2, KEY_ROWS, COLS, WIDTH), BF16),
            pltpu.VMEM((PARTS, 2, 2, EDGE, GW), BF16),
            pltpu.VMEM((PARTS, 2, 2, EDGE, GW), BF16),
            pltpu.VMEM((2, NEAR, HEADS * OWN), F32),
            pltpu.VMEM((2, PARTS * BANDS, NEAR, QL), F32),
            pltpu.VMEM((2, PARTS * BANDS, NEAR, QL), F32),
            pltpu.VMEM((2, PARTS, 16, QL), F32),
            pltpu.VMEM((2, PARTS, 8, QL), F32),
            pltpu.VMEM((PARTS, 2, 3 * BANDS, 128), F32),
            pltpu.VMEM((PARTS, 2, 3 * BANDS, 128), F32),
            pltpu.VMEM((PARTS, 2, 3 * BANDS, 128), F32),
            pltpu.VMEM((PARTS, 2, 3 * BANDS, 128), F32),
            pltpu.VMEM((TOKENS, WIDTH), F32),
            pltpu.VMEM((TOKENS, WIDTH), BF16),
            pltpu.VMEM((PARTS, 1, 2, EDGE, GW), BF16),
            pltpu.VMEM((PARTS, 2, EDGE, GW), BF16),
            pltpu.VMEM((2, KEY_ROWS * COLS, WIDTH), F32),
            pltpu.VMEM((PARTS, 2, 2, RIM, GW), BF16),
            pltpu.VMEM((PARTS, 2, 2, RIM, GW), BF16),
            pltpu.VMEM((128, 128), F32),
            pltpu.VMEM((WINDOW, HEADS, WINDOW), F32),
            dma((PARTS, 16)),
            dma((PARTS, 16)),
            dma((5,)),
        ],
        name="neighbourhood",
        compiler_params=pltpu.CompilerParams(
            collective_id=0, has_side_effects=True, vmem_limit_bytes=40 * 1024 * 1024),
    )(*args)
    return pl.pallas_call(
        hand_on,
        out_shape=(block, block, block),
        in_specs=[vmem] * 3,
        out_specs=(vmem,) * 3,
        name="hand_on",
        compiler_params=pltpu.CompilerParams(vmem_limit_bytes=8 * 1024 * 1024),
    )(*grads)


def solution(mesh):
    spec = P("lat", "lon", None)
    return jax.shard_map(
        functools.partial(on_device, mesh.shape["lat"], mesh.shape["lon"]),
        mesh=mesh,
        in_specs=(spec, spec, spec, spec, P()),
        out_specs=(spec, spec, spec),
        check_vma=False,
    )
```

```python
import functools

import jax
import jax.numpy as jnp
from jax import lax
from jax.experimental import pallas as pl
from jax.experimental.pallas import tpu as pltpu
from jax.sharding import PartitionSpec as P

WINDOW = 13
RADIUS = 6
HEADS = 8
HEAD_DIM = 64
ROWS = 16
COLS = 16
KEY_ROWS = ROWS + 2 * RADIUS
WIDE = 32
BAND = 4
BANDS = ROWS // BAND
DEEP = BAND + 2 * RADIUS
WIDTH = HEADS * HEAD_DIM
OWN = BAND * COLS
NEAR = DEEP * COLS
TOKENS = ROWS * COLS
EDGE = ROWS * RADIUS
RIM = RADIUS * COLS
GROUP = 4
PARTS = HEADS // GROUP
GW = GROUP * HEAD_DIM
QL = GROUP * OWN
SIDE = 8
SL = GROUP * BAND * SIDE
STRIP = 384
NEG = -1e30
MESH = pl.DeviceIdType.MESH
F32 = jnp.float32
BF16 = jnp.bfloat16


def iota(shape, dim):
    return lax.broadcasted_iota(jnp.int32, shape, dim)


def sixth(j):
    return lax.shift_right_logical(j * 10923, 16)


def sel(mask):
    return jnp.where(mask, 1.0, 0.0).astype(BF16)


def onehot(rows, cols, target):
    return sel(target == iota((rows, cols), 1))


def dot(a, b):
    return jnp.dot(a, b, preferred_element_type=F32)


def dot_t(a, b):
    return lax.dot_general(a, b, (((1,), (1,)), ((), ())), preferred_element_type=F32)


def t_dot(a, b):
    return lax.dot_general(a, b, (((0,), (0,)), ((), ())), preferred_element_type=F32)


def dot3(a, pick):
    hi = a.astype(BF16)
    rest = a - hi.astype(F32)
    mid = rest.astype(BF16)
    low = (rest - mid.astype(F32)).astype(BF16)
    return dot(hi, pick) + dot(mid, pick) + dot(low, pick)


def edge_token(j, start):
    r = sixth(j)
    return r * COLS + (j - r * RADIUS) + start


def edge_index(token, west, east):
    r = lax.shift_right_logical(token, 4)
    c = lax.bitwise_and(token, 15)
    at = r * RADIUS + c
    in_west = (c >= west) & (c < west + RADIUS)
    in_east = (c >= east) & (c < east + RADIUS)
    return jnp.where(in_west, at - west, jnp.where(in_east, at - east + EDGE, -1))


def side_lane(j, start):
    c = lax.bitwise_and(j, SIDE - 1)
    return jnp.where(c < RADIUS, lax.shift_right_logical(j, 3) * COLS + c + start, -1)


def pick_lanes(start):
    return sel(iota((QL, SL), 0) == side_lane(iota((QL, SL), 1), start))


def put_lanes(start):
    return sel(iota((SL, QL), 1) == side_lane(iota((SL, QL), 0), start))


def combine(a, b, shared):
    m0 = a[0:BANDS]
    m1 = jnp.where(shared, b[0:BANDS], NEG)
    m = jnp.maximum(m0, m1)
    w0 = jnp.exp(m0 - m)
    w1 = jnp.exp(m1 - m)
    total = a[BANDS:2 * BANDS] * w0 + b[BANDS:2 * BANDS] * w1
    weighed = a[2 * BANDS:] * w0 + b[2 * BANDS:] * w1
    return m + jnp.log(total), weighed / total


def kernel(nlat, nlon, q_ref, k_ref, v_ref, g_ref, bias_ref, dq_ref, dk_ref, dv_ref,
           qg, kv, send, land, table, rim_table, scores, rim_scores, rim_dprobs, dprobs, srow, final,
           psend, pland, osend, oland, own_dq, halo_dq, dsend, dland, acc, lsend, lland,
           biases, bias, ss, rs, ins):
    lat = lax.axis_index("lat")
    lon = lax.axis_index("lon")
    east = (lat, lax.rem(lon + 1, nlon))
    west = (lat, lax.rem(lon + nlon - 1, nlon))
    north = (lat - 1, lon)
    south = (lat + 1, lon)
    has_north = lat > 0
    has_south = lat < nlat - 1

    loads = [pltpu.make_async_copy(ref, dst, ins.at[i]) for i, (ref, dst) in enumerate((
        (q_ref, qg.at[0, pl.ds(0, ROWS), pl.ds(0, COLS)]),
        (g_ref, qg.at[1, pl.ds(0, ROWS), pl.ds(0, COLS)]),
        (k_ref, kv.at[0, pl.ds(RADIUS, ROWS)]),
        (v_ref, kv.at[1, pl.ds(RADIUS, ROWS)]),
        (bias_ref, bias)))]
    for c in loads:
        c.start()

    bar = pltpu.get_barrier_semaphore()
    pl.semaphore_signal(bar, 1, device_id=east, device_id_type=MESH)
    pl.semaphore_signal(bar, 1, device_id=west, device_id_type=MESH)

    @pl.when(has_north)
    def _():
        pl.semaphore_signal(bar, 1, device_id=north, device_id_type=MESH)

    @pl.when(has_south)
    def _():
        pl.semaphore_signal(bar, 1, device_id=south, device_id_type=MESH)

    def lanes(g):
        return slice(g * GW, (g + 1) * GW)

    def pack_edges(dst, t, tokens, starts):
        for d in range(2):
            pick = onehot(EDGE, TOKENS, edge_token(iota((EDGE, TOKENS), 0), starts[d]))
            got = dot(pick, tokens).astype(BF16)
            for g in range(PARTS):
                dst[g, t, d] = got[:, lanes(g)]

    for t in range(2):
        loads[t].wait()
        tokens = qg[t, :, 0:COLS, :].reshape(TOKENS, WIDTH)
        pack_edges(send, t, tokens, (COLS - RADIUS, 0))
    for c in loads[2:]:
        c.wait()
    peers = 2 + has_north.astype(jnp.int32) + has_south.astype(jnp.int32)
    pl.semaphore_wait(bar, peers)

    along = (east, west)
    across = (south, north)

    def remote(g, i, src, dst, to):
        return pltpu.make_async_remote_copy(
            src, dst, ss.at[g, i], rs.at[g, i], device_id=to, device_id_type=MESH)

    def lon_copy(g, t, d):
        return remote(g, 2 * t + d, send.at[g, t, d], land.at[g, t, d], along[d])

    def kv_mid(g):
        span = pl.ds(g * GW, GW)
        return lambda d: [remote(
            g, 4 + 2 * t + d,
            kv.at[t, pl.ds(ROWS if d == 0 else RADIUS, RADIUS), pl.ds(0, COLS), span],
            kv.at[t, pl.ds(0 if d == 0 else ROWS + RADIUS, RADIUS), pl.ds(0, COLS), span],
            across[d]) for t in range(2)]

    def own_copy(g, d):
        return remote(g, 8 + d, osend.at[g, d], oland.at[g, d], along[d])

    def part_copy(g, d):
        return remote(g, 10 + d, psend.at[g, d], pland.at[g, d], along[d])

    def dq_copy(g, d):
        return remote(g, 12 + d, dsend.at[g, 0, d], dland.at[g, d], along[d])

    def lat_back(g):
        return lambda d: [remote(g, 14 + d, lsend.at[g, d], lland.at[g, d], across[d])]

    out_ok = (has_south, has_north)
    in_ok = (has_north, has_south)

    def lat_do(make, ok, what):
        for d in range(2):
            @pl.when(ok[d])
            def _(d=d):
                for c in make(d):
                    what(c)

    def start_lat(make):
        lat_do(make, out_ok, lambda c: c.start())

    def recv_lat(make):
        lat_do(make, in_ok, lambda c: c.wait_recv())

    def sent_lat(make):
        lat_do(make, out_ok, lambda c: c.wait_send())

    def start_lon(g):
        for t in range(2):
            for d in range(2):
                lon_copy(g, t, d).start()

    start_lat(kv_mid(0))
    start_lat(kv_mid(1))
    start_lon(0)
    start_lon(1)

    @pl.when(jnp.logical_not(has_north))
    def _():
        kv[:, 0:RADIUS] = jnp.zeros((2, RADIUS, COLS, WIDTH), BF16)

    @pl.when(jnp.logical_not(has_south))
    def _():
        kv[:, RADIUS + ROWS:KEY_ROWS] = jnp.zeros((2, RADIUS, COLS, WIDTH), BF16)

    acc[...] = jnp.zeros((2, KEY_ROWS, COLS, WIDTH), F32)

    biases[...] = jnp.zeros((128, 128), F32)
    for a in range(WINDOW):
        biases[a * HEADS:(a + 1) * HEADS, 0:WINDOW] = bias[a]
    turned = jnp.transpose(biases[...])[0:16, :]
    row = iota((128, STRIP), 0)
    step = 15 - lax.shift_right_logical(iota((128, STRIP), 1), 4)
    w = lax.shift_right_logical(iota((COLS, STRIP), 1), 4)
    cc = lax.bitwise_and(iota((COLS, STRIP), 1), 15)
    in_window = (w >= 3) & (w < 3 + WINDOW)
    offset = jnp.where(in_window, iota((COLS, STRIP), 0) + RADIUS - cc, -1)
    rim_step = 15 - lax.shift_right_logical(iota((128, 256), 1), 3)
    rim_row = iota((128, 256), 0)
    w = lax.shift_right_logical(iota((2 * SIDE, 256), 1), 3)
    cc = lax.bitwise_and(iota((2 * SIDE, 256), 1), SIDE - 1)
    key_col = iota((2 * SIDE, 256), 0)
    far = jnp.where(key_col < SIDE, cc - RADIUS, cc + COLS)
    rim_known = (w >= 3) & (w < 3 + WINDOW) & (cc < RADIUS)
    rim_offset = jnp.where(rim_known, key_col - far + RADIUS, -1)
    for h in range(HEADS):
        spread = dot3(turned, sel(row == step * HEADS + h))
        strip = jnp.full((COLS, STRIP), NEG, F32)
        for b in range(WINDOW):
            strip = jnp.where(offset == b, spread[b:b + 1, :], strip)
        for r in range(DEEP):
            shift = (DEEP - 1 - r) * COLS
            moved = pltpu.roll(strip, STRIP - shift, 1) if shift else strip
            table[r * COLS:(r + 1) * COLS, h * OWN:(h + 1) * OWN] = moved[:, :OWN]
        spread = dot3(turned, sel(rim_row == rim_step * HEADS + h))
        strip = jnp.full((2 * SIDE, 256), NEG, F32)
        for b in range(WINDOW):
            strip = jnp.where(rim_offset == b, spread[b:b + 1, :], strip)
        for r in range(DEEP):
            shift = (DEEP - 1 - r) * SIDE
            moved = pltpu.roll(strip, 256 - shift, 1) if shift else strip
            for side in range(2):
                rim_table[side, r * SIDE:(r + 1) * SIDE, h * 32:(h + 1) * 32] = (
                    moved[side * SIDE:(side + 1) * SIDE, :32])

    head_of = lax.shift_right_logical(iota((1, GW), 1), 6)
    keep = [jnp.where(head_of == hh, 1.0, 0.0) for hh in range(GROUP)]
    keep_low = [m.astype(BF16) for m in keep]
    scale = HEAD_DIM ** -0.5

    def stack(x):
        return jnp.concatenate([x * m for m in keep_low], axis=0)

    def unstack(y):
        n = y.shape[0] // GROUP
        total = y[0:n] * keep[0]
        for hh in range(1, GROUP):
            total = total + y[hh * n:(hh + 1) * n] * keep[hh]
        return total

    def side_of(x, side):
        rows = x.shape[0] * SIDE
        return x.astype(F32)[:, side * SIDE:(side + 1) * SIDE, :].reshape(rows, GW)

    def operands(half, g, lo):
        cols = pl.ds(half * COLS, COLS)
        tiles = (qg[0, lo:lo + BAND, cols, lanes(g)], qg[1, lo:lo + BAND, cols, lanes(g)],
                 kv[0, lo:lo + DEEP, :, lanes(g)], kv[1, lo:lo + DEEP, :, lanes(g)])
        if half:
            sets = [[side_of(x, side) for x in tiles] for side in range(2)]
        else:
            sets = [[x.reshape(x.shape[0] * COLS, GW) for x in tiles]]
        return [(stack((q * scale).astype(BF16)), stack(g.astype(BF16)), k.astype(BF16),
                 v.astype(BF16)) for q, g, k, v in sets]

    hide_north = jnp.where(has_north, 0.0, NEG)
    hide_south = jnp.where(has_south, 0.0, NEG)

    def score(half, g):
        for band in range(BANDS):
            lo = band * BAND
            for side, (qs, gs, kt, vt) in enumerate(operands(half, g, lo)):
                if half:
                    bias_of = rim_table[side, :, g * SL:(g + 1) * SL]
                else:
                    bias_of = table[:, g * QL:(g + 1) * QL]
                s = dot_t(kt, qs) + bias_of
                width = kt.shape[0] // DEEP
                above = max(RADIUS - lo, 0) * width
                below = min(RADIUS + ROWS - lo, DEEP) * width
                if above:
                    s = jnp.concatenate([s[:above] + hide_north, s[above:]], axis=0)
                if below < DEEP * width:
                    s = jnp.concatenate([s[:below], s[below:] + hide_south], axis=0)
                dp = dot_t(vt, gs)
                if half:
                    rim_scores[g * BANDS + band, side] = s
                    rim_dprobs[g * BANDS + band, side] = dp
                else:
                    scores[g * BANDS + band] = s
                    dprobs[g * BANDS + band] = dp
                m = jnp.max(s, axis=0, keepdims=True)
                e = jnp.exp(s - m)
                at = slice(side * SL, side * SL + s.shape[1])
                srow[half, g, band:band + 1, at] = m
                srow[half, g, BANDS + band:BANDS + band + 1, at] = jnp.sum(
                    e, axis=0, keepdims=True)
                srow[half, g, 2 * BANDS + band:2 * BANDS + band + 1, at] = jnp.sum(
                    e * dp, axis=0, keepdims=True)
        return srow[half, g, 0:3 * BANDS, :]

    def grad(half, g):
        for band in range(BANDS):
            lo = band * BAND
            dqs = []
            for side, (qs, gs, kt, _) in enumerate(operands(half, g, lo)):
                at = slice(side * SL, side * SL + qs.shape[0])
                lse = final[half, g, band:band + 1, at]
                delta = final[half, g, BANDS + band:BANDS + band + 1, at]
                if half:
                    s, dp = rim_scores[g * BANDS + band, side], rim_dprobs[g * BANDS + band, side]
                else:
                    s, dp = scores[g * BANDS + band], dprobs[g * BANDS + band]
                p = jnp.exp(s - lse)
                ds = (p * (dp - delta)).astype(BF16)
                width = kt.shape[0] // DEEP
                cols = slice(side * SIDE, side * SIDE + width)
                dk, dv = dot(ds, qs), dot(p.astype(BF16), gs)
                acc[0, lo:lo + DEEP, cols, lanes(g)] += dk.reshape(DEEP, width, GW)
                acc[1, lo:lo + DEEP, cols, lanes(g)] += dv.reshape(DEEP, width, GW)
                dqs.append((unstack(t_dot(ds, kt)) * scale).reshape(BAND, width, GW))
            if half:
                both = jnp.concatenate(dqs, axis=1)
                halo_dq[band * OWN:(band + 1) * OWN, lanes(g)] = both.reshape(OWN, GW).astype(BF16)
            else:
                own_dq[band * OWN:(band + 1) * OWN, lanes(g)] = dqs[0].reshape(OWN, GW)

    column = lax.bitwise_and(iota((BANDS, QL), 1), 15)
    spread_lon = onehot(TOKENS, 2 * EDGE, edge_index(iota((TOKENS, 2 * EDGE), 0), 0, SIDE))
    mine = {}
    parts = {}

    def own_scores(g):
        recv_lat(kv_mid(g))
        mine[g] = score(0, g)
        for d in range(2):
            osend[g, d] = dot3(mine[g], pick_lanes(COLS - RADIUS if d == 0 else 0))
        for d in range(2):
            own_copy(g, d).start()

    def halo_scores(g):
        for t in range(2):
            for d in range(2):
                lon_copy(g, t, d).wait_recv()
            got = dot(spread_lon, land[g, t].reshape(2 * EDGE, GW)).astype(BF16)
            qg[t, :, COLS:WIDE, lanes(g)] = got.reshape(ROWS, 16, GW)
        parts[g] = score(1, g)
        for d in range(2):
            psend[g, d] = parts[g][:, (1 - d) * SL:(2 - d) * SL]
        for d in range(2):
            part_copy(g, d).start()

    def halo_grads(g):
        for d in range(2):
            own_copy(g, d).wait_recv()
        theirs = jnp.concatenate([oland[g, 0], oland[g, 1]], axis=1)
        held = lax.bitwise_and(iota((BANDS, QL), 1), SIDE - 1) < RADIUS
        lse, delta = combine(parts[g], theirs, held)
        final[1, g, 0:BANDS, :] = jnp.where(held, lse, 0.0)
        final[1, g, BANDS:2 * BANDS, :] = jnp.where(held, delta, 0.0)
        grad(1, g)
        for d in range(2):
            start = SIDE if d == 0 else 0
            pick = onehot(EDGE, TOKENS, edge_token(iota((EDGE, TOKENS), 0), start))
            dsend[g, 0, d] = dot(pick, halo_dq[:, lanes(g)]).astype(BF16)
        for d in range(2):
            dq_copy(g, d).start()

    def own_grads(g):
        theirs = jnp.zeros((3 * BANDS, QL), F32)
        for d in range(2):
            part_copy(g, d).wait_recv()
            theirs = theirs + dot3(pland[g, d], put_lanes(0 if d == 0 else COLS - RADIUS))
        lse, delta = combine(mine[g], theirs, (column < RADIUS) | (column >= COLS - RADIUS))
        final[0, g, 0:BANDS, :] = lse
        final[0, g, BANDS:2 * BANDS, :] = delta
        grad(0, g)
        for t in range(2):
            last = acc[t, RADIUS + ROWS:, :, lanes(g)]
            lsend[g, 0, t] = last.reshape(RIM, GW).astype(BF16)
            lsend[g, 1, t] = acc[t, 0:RADIUS, :, lanes(g)].reshape(RIM, GW).astype(BF16)
        start_lat(lat_back(g))

    own_scores(0)
    own_scores(1)
    halo_scores(0)
    halo_scores(1)
    halo_grads(0)
    halo_grads(1)
    own_grads(0)
    own_grads(1)

    spread_dq = onehot(TOKENS, 2 * EDGE,
                       edge_index(iota((TOKENS, 2 * EDGE), 0), 0, COLS - RADIUS))
    for g in range(PARTS):
        for d in range(2):
            dq_copy(g, d).wait_recv()
        dq = own_dq[:, lanes(g)] + dot(spread_dq, dland[g].reshape(2 * EDGE, GW))
        dq_ref[:, :, lanes(g)] = dq.astype(BF16).reshape(ROWS, COLS, GW)
    for g in range(PARTS):
        recv_lat(lat_back(g))
        for t, out in enumerate((dk_ref, dv_ref)):
            first, last = RADIUS, RADIUS + ROWS
            rim = (RADIUS, COLS, GW)
            top = lland[g, 0, t].astype(F32).reshape(rim)
            top = acc[t, first:first + RADIUS, :, lanes(g)] + jnp.where(has_north, top, 0.0)
            bottom = lland[g, 1, t].astype(F32).reshape(rim)
            bottom = acc[t, last - RADIUS:last, :, lanes(g)] + jnp.where(has_south, bottom, 0.0)
            middle = acc[t, first + RADIUS:last - RADIUS, :, lanes(g)]
            out[0:RADIUS, :, lanes(g)] = top.astype(BF16)
            out[RADIUS:ROWS - RADIUS, :, lanes(g)] = middle.astype(BF16)
            out[ROWS - RADIUS:ROWS, :, lanes(g)] = bottom.astype(BF16)

    for g in range(PARTS):
        for d in range(2):
            for t in range(2):
                lon_copy(g, t, d).wait_send()
            own_copy(g, d).wait_send()
            part_copy(g, d).wait_send()
            dq_copy(g, d).wait_send()
        sent_lat(kv_mid(g))
        sent_lat(lat_back(g))


def hand_on(*refs):
    copies = [pltpu.make_async_copy(refs[i], refs[3 + i], refs[6].at[i]) for i in range(3)]
    for c in copies:
        c.start()
    for c in copies:
        c.wait()


def on_device(nlat, nlon, queries, keys, values, out_grad, pos_bias):
    block = jax.ShapeDtypeStruct((ROWS, COLS, WIDTH), BF16)
    vmem = pl.BlockSpec(memory_space=pltpu.VMEM)
    dma = pltpu.SemaphoreType.DMA
    args = (queries, keys, values, out_grad, jnp.transpose(pos_bias, (1, 0, 2)))
    args = [pltpu.with_memory_space_constraint(x, pltpu.HBM) for x in args]
    grads = pl.pallas_call(
        functools.partial(kernel, nlat, nlon),
        out_shape=(block, block, block),
        in_specs=[pl.BlockSpec(memory_space=pltpu.HBM)] * 5,
        out_specs=(vmem,) * 3,
        scratch_shapes=[
            pltpu.VMEM((2, ROWS, WIDE, WIDTH), BF16),
            pltpu.VMEM((2, KEY_ROWS, COLS, WIDTH), BF16),
            pltpu.VMEM((PARTS, 2, 2, EDGE, GW), BF16),
            pltpu.VMEM((PARTS, 2, 2, EDGE, GW), BF16),
            pltpu.VMEM((NEAR, HEADS * OWN), F32),
            pltpu.VMEM((2, DEEP * SIDE, HEADS * BAND * SIDE), F32),
            pltpu.VMEM((PARTS * BANDS, NEAR, QL), F32),
            pltpu.VMEM((PARTS * BANDS, 2, DEEP * SIDE, SL), F32),
            pltpu.VMEM((PARTS * BANDS, 2, DEEP * SIDE, SL), F32),
            pltpu.VMEM((PARTS * BANDS, NEAR, QL), F32),
            pltpu.VMEM((2, PARTS, 16, QL), F32),
            pltpu.VMEM((2, PARTS, 8, QL), F32),
            pltpu.VMEM((PARTS, 2, 3 * BANDS, 128), F32),
            pltpu.VMEM((PARTS, 2, 3 * BANDS, 128), F32),
            pltpu.VMEM((PARTS, 2, 3 * BANDS, 128), F32),
            pltpu.VMEM((PARTS, 2, 3 * BANDS, 128), F32),
            pltpu.VMEM((TOKENS, WIDTH), F32),
            pltpu.VMEM((TOKENS, WIDTH), BF16),
            pltpu.VMEM((PARTS, 1, 2, EDGE, GW), BF16),
            pltpu.VMEM((PARTS, 2, EDGE, GW), BF16),
            pltpu.VMEM((2, KEY_ROWS, COLS, WIDTH), F32),
            pltpu.VMEM((PARTS, 2, 2, RIM, GW), BF16),
            pltpu.VMEM((PARTS, 2, 2, RIM, GW), BF16),
            pltpu.VMEM((128, 128), F32),
            pltpu.VMEM((WINDOW, HEADS, WINDOW), F32),
            dma((PARTS, 16)),
            dma((PARTS, 16)),
            dma((5,)),
        ],
        name="neighbourhood",
        compiler_params=pltpu.CompilerParams(
            collective_id=0, has_side_effects=True, vmem_limit_bytes=40 * 1024 * 1024),
    )(*args)
    return pl.pallas_call(
        hand_on,
        out_shape=(block, block, block),
        in_specs=[vmem] * 3,
        out_specs=(pl.BlockSpec(memory_space=pltpu.HBM),) * 3,
        scratch_shapes=[dma((3,))],
        name="hand_on",
        compiler_params=pltpu.CompilerParams(vmem_limit_bytes=8 * 1024 * 1024),
    )(*grads)


def solution(mesh):
    spec = P("lat", "lon", None)
    return jax.shard_map(
        functools.partial(on_device, mesh.shape["lat"], mesh.shape["lon"]),
        mesh=mesh,
        in_specs=(spec, spec, spec, spec, P()),
        out_specs=(spec, spec, spec),
        check_vma=False,
    )
```

```python
import functools

import jax
import jax.numpy as jnp
from jax import lax
from jax.experimental import pallas as pl
from jax.experimental.pallas import tpu as pltpu
from jax.sharding import PartitionSpec as P

WINDOW = 13
RADIUS = 6
HEADS = 8
HEAD_DIM = 64
ROWS = 16
COLS = 16
KEY_ROWS = ROWS + 2 * RADIUS
WIDE = 32
BAND = 4
BANDS = ROWS // BAND
DEEP = BAND + 2 * RADIUS
WIDTH = HEADS * HEAD_DIM
OWN = BAND * COLS
NEAR = DEEP * COLS
TOKENS = ROWS * COLS
EDGE = ROWS * RADIUS
RIM = RADIUS * COLS
GROUP = 4
PARTS = HEADS // GROUP
GW = GROUP * HEAD_DIM
QL = GROUP * OWN
SIDE = 8
SL = GROUP * BAND * SIDE
STRIP = 384
NEG = -1e30
MESH = pl.DeviceIdType.MESH
F32 = jnp.float32
BF16 = jnp.bfloat16


def iota(shape, dim):
    return lax.broadcasted_iota(jnp.int32, shape, dim)


def sixth(j):
    return lax.shift_right_logical(j * 10923, 16)


def sel(mask):
    return jnp.where(mask, 1.0, 0.0).astype(BF16)


def onehot(rows, cols, target):
    return sel(target == iota((rows, cols), 1))


def dot(a, b):
    return jnp.dot(a, b, preferred_element_type=F32)


def dot_t(a, b):
    return lax.dot_general(a, b, (((1,), (1,)), ((), ())), preferred_element_type=F32)


def t_dot(a, b):
    return lax.dot_general(a, b, (((0,), (0,)), ((), ())), preferred_element_type=F32)


def dot3(a, pick):
    hi = a.astype(BF16)
    rest = a - hi.astype(F32)
    mid = rest.astype(BF16)
    low = (rest - mid.astype(F32)).astype(BF16)
    return dot(hi, pick) + dot(mid, pick) + dot(low, pick)


def edge_token(j, start):
    r = sixth(j)
    return r * COLS + (j - r * RADIUS) + start


def edge_index(token, west, east):
    r = lax.shift_right_logical(token, 4)
    c = lax.bitwise_and(token, 15)
    at = r * RADIUS + c
    in_west = (c >= west) & (c < west + RADIUS)
    in_east = (c >= east) & (c < east + RADIUS)
    return jnp.where(in_west, at - west, jnp.where(in_east, at - east + EDGE, -1))


def side_lane(j, start):
    c = lax.bitwise_and(j, SIDE - 1)
    return jnp.where(c < RADIUS, lax.shift_right_logical(j, 3) * COLS + c + start, -1)


def pick_lanes(start):
    return sel(iota((QL, SL), 0) == side_lane(iota((QL, SL), 1), start))


def put_lanes(start):
    return sel(iota((SL, QL), 1) == side_lane(iota((SL, QL), 0), start))


def combine(a, b, shared):
    m0 = a[0:BANDS]
    m1 = jnp.where(shared, b[0:BANDS], NEG)
    m = jnp.maximum(m0, m1)
    w0 = jnp.exp(m0 - m)
    w1 = jnp.exp(m1 - m)
    total = a[BANDS:2 * BANDS] * w0 + b[BANDS:2 * BANDS] * w1
    weighed = a[2 * BANDS:] * w0 + b[2 * BANDS:] * w1
    return m + jnp.log(total), weighed / total


def kernel(nlat, nlon, q_ref, k_ref, v_ref, g_ref, bias_ref, dq_ref, dk_ref, dv_ref,
           qg, kv, send, land, table, rim_table, scores, rim_scores, rim_dprobs, dprobs, srow, final,
           psend, pland, osend, oland, own_dq, halo_dq, dsend, dland, acc, lsend, lland,
           biases, bias, ss, rs, ins):
    lat = lax.axis_index("lat")
    lon = lax.axis_index("lon")
    east = (lat, lax.rem(lon + 1, nlon))
    west = (lat, lax.rem(lon + nlon - 1, nlon))
    north = (lat - 1, lon)
    south = (lat + 1, lon)
    has_north = lat > 0
    has_south = lat < nlat - 1

    loads = [pltpu.make_async_copy(ref, dst, ins.at[i]) for i, (ref, dst) in enumerate((
        (q_ref, qg.at[0, pl.ds(0, ROWS), pl.ds(0, COLS)]),
        (g_ref, qg.at[1, pl.ds(0, ROWS), pl.ds(0, COLS)]),
        (k_ref, kv.at[0, pl.ds(RADIUS, ROWS)]),
        (v_ref, kv.at[1, pl.ds(RADIUS, ROWS)]),
        (bias_ref, bias)))]
    for c in loads:
        c.start()

    bar = pltpu.get_barrier_semaphore()
    pl.semaphore_signal(bar, 1, device_id=east, device_id_type=MESH)
    pl.semaphore_signal(bar, 1, device_id=west, device_id_type=MESH)

    @pl.when(has_north)
    def _():
        pl.semaphore_signal(bar, 1, device_id=north, device_id_type=MESH)

    @pl.when(has_south)
    def _():
        pl.semaphore_signal(bar, 1, device_id=south, device_id_type=MESH)

    def lanes(g):
        return slice(g * GW, (g + 1) * GW)

    def pack_edges(dst, t, tokens, starts):
        for d in range(2):
            pick = onehot(EDGE, TOKENS, edge_token(iota((EDGE, TOKENS), 0), starts[d]))
            got = dot(pick, tokens).astype(BF16)
            for g in range(PARTS):
                dst[g, t, d] = got[:, lanes(g)]

    along = (east, west)
    across = (south, north)

    def remote(g, i, src, dst, to):
        return pltpu.make_async_remote_copy(
            src, dst, ss.at[g, i], rs.at[g, i], device_id=to, device_id_type=MESH)

    def lon_copy(g, t, d):
        return remote(g, 2 * t + d, send.at[g, t, d], land.at[g, t, d], along[d])

    def kv_mid(g):
        span = pl.ds(g * GW, GW)
        return lambda d: [remote(
            g, 4 + 2 * t + d,
            kv.at[t, pl.ds(ROWS if d == 0 else RADIUS, RADIUS), pl.ds(0, COLS), span],
            kv.at[t, pl.ds(0 if d == 0 else ROWS + RADIUS, RADIUS), pl.ds(0, COLS), span],
            across[d]) for t in range(2)]

    def own_copy(g, d):
        return remote(g, 8 + d, osend.at[g, d], oland.at[g, d], along[d])

    def part_copy(g, d):
        return remote(g, 10 + d, psend.at[g, d], pland.at[g, d], along[d])

    def dq_copy(g, d):
        return remote(g, 12 + d, dsend.at[g, 0, d], dland.at[g, d], along[d])

    def lat_back(g):
        return lambda d: [remote(g, 14 + d, lsend.at[g, d], lland.at[g, d], across[d])]

    out_ok = (has_south, has_north)
    in_ok = (has_north, has_south)

    def lat_do(make, ok, what):
        for d in range(2):
            @pl.when(ok[d])
            def _(d=d):
                for c in make(d):
                    what(c)

    def start_lat(make):
        lat_do(make, out_ok, lambda c: c.start())

    def recv_lat(make):
        lat_do(make, in_ok, lambda c: c.wait_recv())

    def sent_lat(make):
        lat_do(make, out_ok, lambda c: c.wait_send())

    def start_lon(g):
        for t in range(2):
            for d in range(2):
                lon_copy(g, t, d).start()

    for c in loads[2:]:
        c.wait()
    peers = 2 + has_north.astype(jnp.int32) + has_south.astype(jnp.int32)
    pl.semaphore_wait(bar, peers)
    start_lat(kv_mid(0))
    start_lat(kv_mid(1))
    for t in range(2):
        loads[t].wait()
        tokens = qg[t, :, 0:COLS, :].reshape(TOKENS, WIDTH)
        pack_edges(send, t, tokens, (COLS - RADIUS, 0))
    start_lon(0)
    start_lon(1)

    @pl.when(jnp.logical_not(has_north))
    def _():
        kv[:, 0:RADIUS] = jnp.zeros((2, RADIUS, COLS, WIDTH), BF16)

    @pl.when(jnp.logical_not(has_south))
    def _():
        kv[:, RADIUS + ROWS:KEY_ROWS] = jnp.zeros((2, RADIUS, COLS, WIDTH), BF16)

    acc[...] = jnp.zeros((2, KEY_ROWS, COLS, WIDTH), F32)

    biases[...] = jnp.zeros((128, 128), F32)
    for a in range(WINDOW):
        biases[a * HEADS:(a + 1) * HEADS, 0:WINDOW] = bias[a]
    turned = jnp.transpose(biases[...])[0:16, :]
    row = iota((128, STRIP), 0)
    step = 15 - lax.shift_right_logical(iota((128, STRIP), 1), 4)
    w = lax.shift_right_logical(iota((COLS, STRIP), 1), 4)
    cc = lax.bitwise_and(iota((COLS, STRIP), 1), 15)
    in_window = (w >= 3) & (w < 3 + WINDOW)
    offset = jnp.where(in_window, iota((COLS, STRIP), 0) + RADIUS - cc, -1)
    rim_step = 15 - lax.shift_right_logical(iota((128, 256), 1), 3)
    rim_row = iota((128, 256), 0)
    w = lax.shift_right_logical(iota((2 * SIDE, 256), 1), 3)
    cc = lax.bitwise_and(iota((2 * SIDE, 256), 1), SIDE - 1)
    key_col = iota((2 * SIDE, 256), 0)
    far = jnp.where(key_col < SIDE, cc - RADIUS, cc + COLS)
    rim_known = (w >= 3) & (w < 3 + WINDOW) & (cc < RADIUS)
    rim_offset = jnp.where(rim_known, key_col - far + RADIUS, -1)
    for h in range(HEADS):
        spread = dot3(turned, sel(row == step * HEADS + h))
        strip = jnp.full((COLS, STRIP), NEG, F32)
        for b in range(WINDOW):
            strip = jnp.where(offset == b, spread[b:b + 1, :], strip)
        for r in range(DEEP):
            shift = (DEEP - 1 - r) * COLS
            moved = pltpu.roll(strip, STRIP - shift, 1) if shift else strip
            table[r * COLS:(r + 1) * COLS, h * OWN:(h + 1) * OWN] = moved[:, :OWN]
        spread = dot3(turned, sel(rim_row == rim_step * HEADS + h))
        strip = jnp.full((2 * SIDE, 256), NEG, F32)
        for b in range(WINDOW):
            strip = jnp.where(rim_offset == b, spread[b:b + 1, :], strip)
        for r in range(DEEP):
            shift = (DEEP - 1 - r) * SIDE
            moved = pltpu.roll(strip, 256 - shift, 1) if shift else strip
            for side in range(2):
                rim_table[side, r * SIDE:(r + 1) * SIDE, h * 32:(h + 1) * 32] = (
                    moved[side * SIDE:(side + 1) * SIDE, :32])

    head_of = lax.shift_right_logical(iota((1, GW), 1), 6)
    keep = [jnp.where(head_of == hh, 1.0, 0.0) for hh in range(GROUP)]
    keep_low = [m.astype(BF16) for m in keep]
    scale = HEAD_DIM ** -0.5

    def stack(x):
        return jnp.concatenate([x * m for m in keep_low], axis=0)

    def unstack(y):
        n = y.shape[0] // GROUP
        total = y[0:n] * keep[0]
        for hh in range(1, GROUP):
            total = total + y[hh * n:(hh + 1) * n] * keep[hh]
        return total

    def side_of(x, side):
        rows = x.shape[0] * SIDE
        return x.astype(F32)[:, side * SIDE:(side + 1) * SIDE, :].reshape(rows, GW)

    def operands(half, g, lo):
        cols = pl.ds(half * COLS, COLS)
        tiles = (qg[0, lo:lo + BAND, cols, lanes(g)], qg[1, lo:lo + BAND, cols, lanes(g)],
                 kv[0, lo:lo + DEEP, :, lanes(g)], kv[1, lo:lo + DEEP, :, lanes(g)])
        if half:
            sets = [[side_of(x, side) for x in tiles] for side in range(2)]
        else:
            sets = [[x.reshape(x.shape[0] * COLS, GW) for x in tiles]]
        return [(stack((q * scale).astype(BF16)), stack(g.astype(BF16)), k.astype(BF16),
                 v.astype(BF16)) for q, g, k, v in sets]

    hide_north = jnp.where(has_north, 0.0, NEG)
    hide_south = jnp.where(has_south, 0.0, NEG)

    def score(half, g):
        for band in range(BANDS):
            lo = band * BAND
            for side, (qs, gs, kt, vt) in enumerate(operands(half, g, lo)):
                if half:
                    bias_of = rim_table[side, :, g * SL:(g + 1) * SL]
                else:
                    bias_of = table[:, g * QL:(g + 1) * QL]
                s = dot_t(kt, qs) + bias_of
                width = kt.shape[0] // DEEP
                above = max(RADIUS - lo, 0) * width
                below = min(RADIUS + ROWS - lo, DEEP) * width
                if above:
                    s = jnp.concatenate([s[:above] + hide_north, s[above:]], axis=0)
                if below < DEEP * width:
                    s = jnp.concatenate([s[:below], s[below:] + hide_south], axis=0)
                dp = dot_t(vt, gs)
                if half:
                    rim_scores[g * BANDS + band, side] = s
                    rim_dprobs[g * BANDS + band, side] = dp
                else:
                    scores[g * BANDS + band] = s
                    dprobs[g * BANDS + band] = dp
                m = jnp.max(s, axis=0, keepdims=True)
                e = jnp.exp(s - m)
                at = slice(side * SL, side * SL + s.shape[1])
                srow[half, g, band:band + 1, at] = m
                srow[half, g, BANDS + band:BANDS + band + 1, at] = jnp.sum(
                    e, axis=0, keepdims=True)
                srow[half, g, 2 * BANDS + band:2 * BANDS + band + 1, at] = jnp.sum(
                    e * dp, axis=0, keepdims=True)
        return srow[half, g, 0:3 * BANDS, :]

    def grad(half, g):
        for band in range(BANDS):
            lo = band * BAND
            dqs = []
            for side, (qs, gs, kt, _) in enumerate(operands(half, g, lo)):
                at = slice(side * SL, side * SL + qs.shape[0])
                lse = final[half, g, band:band + 1, at]
                delta = final[half, g, BANDS + band:BANDS + band + 1, at]
                if half:
                    s, dp = rim_scores[g * BANDS + band, side], rim_dprobs[g * BANDS + band, side]
                else:
                    s, dp = scores[g * BANDS + band], dprobs[g * BANDS + band]
                p = jnp.exp(s - lse)
                ds = (p * (dp - delta)).astype(BF16)
                width = kt.shape[0] // DEEP
                cols = slice(side * SIDE, side * SIDE + width)
                dk, dv = dot(ds, qs), dot(p.astype(BF16), gs)
                acc[0, lo:lo + DEEP, cols, lanes(g)] += dk.reshape(DEEP, width, GW)
                acc[1, lo:lo + DEEP, cols, lanes(g)] += dv.reshape(DEEP, width, GW)
                dqs.append((unstack(t_dot(ds, kt)) * scale).reshape(BAND, width, GW))
            if half:
                both = jnp.concatenate(dqs, axis=1)
                halo_dq[band * OWN:(band + 1) * OWN, lanes(g)] = both.reshape(OWN, GW).astype(BF16)
            else:
                own_dq[band * OWN:(band + 1) * OWN, lanes(g)] = dqs[0].reshape(OWN, GW)

    column = lax.bitwise_and(iota((BANDS, QL), 1), 15)
    spread_lon = onehot(TOKENS, 2 * EDGE, edge_index(iota((TOKENS, 2 * EDGE), 0), 0, SIDE))
    mine = {}
    parts = {}

    def own_scores(g):
        recv_lat(kv_mid(g))
        mine[g] = score(0, g)
        for d in range(2):
            osend[g, d] = dot3(mine[g], pick_lanes(COLS - RADIUS if d == 0 else 0))
        for d in range(2):
            own_copy(g, d).start()

    def halo_scores(g):
        for t in range(2):
            for d in range(2):
                lon_copy(g, t, d).wait_recv()
            got = dot(spread_lon, land[g, t].reshape(2 * EDGE, GW)).astype(BF16)
            qg[t, :, COLS:WIDE, lanes(g)] = got.reshape(ROWS, 16, GW)
        parts[g] = score(1, g)
        for d in range(2):
            psend[g, d] = parts[g][:, (1 - d) * SL:(2 - d) * SL]
        for d in range(2):
            part_copy(g, d).start()

    def halo_grads(g):
        for d in range(2):
            own_copy(g, d).wait_recv()
        theirs = jnp.concatenate([oland[g, 0], oland[g, 1]], axis=1)
        held = lax.bitwise_and(iota((BANDS, QL), 1), SIDE - 1) < RADIUS
        lse, delta = combine(parts[g], theirs, held)
        final[1, g, 0:BANDS, :] = jnp.where(held, lse, 0.0)
        final[1, g, BANDS:2 * BANDS, :] = jnp.where(held, delta, 0.0)
        grad(1, g)
        for d in range(2):
            start = SIDE if d == 0 else 0
            pick = onehot(EDGE, TOKENS, edge_token(iota((EDGE, TOKENS), 0), start))
            dsend[g, 0, d] = dot(pick, halo_dq[:, lanes(g)]).astype(BF16)
        for d in range(2):
            dq_copy(g, d).start()

    def own_grads(g):
        theirs = jnp.zeros((3 * BANDS, QL), F32)
        for d in range(2):
            part_copy(g, d).wait_recv()
            theirs = theirs + dot3(pland[g, d], put_lanes(0 if d == 0 else COLS - RADIUS))
        lse, delta = combine(mine[g], theirs, (column < RADIUS) | (column >= COLS - RADIUS))
        final[0, g, 0:BANDS, :] = lse
        final[0, g, BANDS:2 * BANDS, :] = delta
        grad(0, g)
        for t in range(2):
            last = acc[t, RADIUS + ROWS:, :, lanes(g)]
            lsend[g, 0, t] = last.reshape(RIM, GW).astype(BF16)
            lsend[g, 1, t] = acc[t, 0:RADIUS, :, lanes(g)].reshape(RIM, GW).astype(BF16)
        start_lat(lat_back(g))

    own_scores(0)
    own_scores(1)
    halo_scores(0)
    halo_scores(1)
    halo_grads(0)
    halo_grads(1)
    own_grads(0)
    own_grads(1)

    spread_dq = onehot(TOKENS, 2 * EDGE,
                       edge_index(iota((TOKENS, 2 * EDGE), 0), 0, COLS - RADIUS))
    for g in range(PARTS):
        for d in range(2):
            dq_copy(g, d).wait_recv()
        dq = own_dq[:, lanes(g)] + dot(spread_dq, dland[g].reshape(2 * EDGE, GW))
        dq_ref[:, :, lanes(g)] = dq.astype(BF16).reshape(ROWS, COLS, GW)
    for g in range(PARTS):
        recv_lat(lat_back(g))
        for t, out in enumerate((dk_ref, dv_ref)):
            first, last = RADIUS, RADIUS + ROWS
            rim = (RADIUS, COLS, GW)
            top = lland[g, 0, t].astype(F32).reshape(rim)
            top = acc[t, first:first + RADIUS, :, lanes(g)] + jnp.where(has_north, top, 0.0)
            bottom = lland[g, 1, t].astype(F32).reshape(rim)
            bottom = acc[t, last - RADIUS:last, :, lanes(g)] + jnp.where(has_south, bottom, 0.0)
            middle = acc[t, first + RADIUS:last - RADIUS, :, lanes(g)]
            out[0:RADIUS, :, lanes(g)] = top.astype(BF16)
            out[RADIUS:ROWS - RADIUS, :, lanes(g)] = middle.astype(BF16)
            out[ROWS - RADIUS:ROWS, :, lanes(g)] = bottom.astype(BF16)

    for g in range(PARTS):
        for d in range(2):
            for t in range(2):
                lon_copy(g, t, d).wait_send()
            own_copy(g, d).wait_send()
            part_copy(g, d).wait_send()
            dq_copy(g, d).wait_send()
        sent_lat(kv_mid(g))
        sent_lat(lat_back(g))


def hand_on(*refs):
    copies = [pltpu.make_async_copy(refs[i], refs[3 + i], refs[6].at[i]) for i in range(3)]
    for c in copies:
        c.start()
    for c in copies:
        c.wait()


def on_device(nlat, nlon, queries, keys, values, out_grad, pos_bias):
    block = jax.ShapeDtypeStruct((ROWS, COLS, WIDTH), BF16)
    vmem = pl.BlockSpec(memory_space=pltpu.VMEM)
    dma = pltpu.SemaphoreType.DMA
    args = (queries, keys, values, out_grad, jnp.transpose(pos_bias, (1, 0, 2)))
    args = [pltpu.with_memory_space_constraint(x, pltpu.HBM) for x in args]
    grads = pl.pallas_call(
        functools.partial(kernel, nlat, nlon),
        out_shape=(block, block, block),
        in_specs=[pl.BlockSpec(memory_space=pltpu.HBM)] * 5,
        out_specs=(vmem,) * 3,
        scratch_shapes=[
            pltpu.VMEM((2, ROWS, WIDE, WIDTH), BF16),
            pltpu.VMEM((2, KEY_ROWS, COLS, WIDTH), BF16),
            pltpu.VMEM((PARTS, 2, 2, EDGE, GW), BF16),
            pltpu.VMEM((PARTS, 2, 2, EDGE, GW), BF16),
            pltpu.VMEM((NEAR, HEADS * OWN), F32),
            pltpu.VMEM((2, DEEP * SIDE, HEADS * BAND * SIDE), F32),
            pltpu.VMEM((PARTS * BANDS, NEAR, QL), F32),
            pltpu.VMEM((PARTS * BANDS, 2, DEEP * SIDE, SL), F32),
            pltpu.VMEM((PARTS * BANDS, 2, DEEP * SIDE, SL), F32),
            pltpu.VMEM((PARTS * BANDS, NEAR, QL), F32),
            pltpu.VMEM((2, PARTS, 16, QL), F32),
            pltpu.VMEM((2, PARTS, 8, QL), F32),
            pltpu.VMEM((PARTS, 2, 3 * BANDS, 128), F32),
            pltpu.VMEM((PARTS, 2, 3 * BANDS, 128), F32),
            pltpu.VMEM((PARTS, 2, 3 * BANDS, 128), F32),
            pltpu.VMEM((PARTS, 2, 3 * BANDS, 128), F32),
            pltpu.VMEM((TOKENS, WIDTH), F32),
            pltpu.VMEM((TOKENS, WIDTH), BF16),
            pltpu.VMEM((PARTS, 1, 2, EDGE, GW), BF16),
            pltpu.VMEM((PARTS, 2, EDGE, GW), BF16),
            pltpu.VMEM((2, KEY_ROWS, COLS, WIDTH), F32),
            pltpu.VMEM((PARTS, 2, 2, RIM, GW), BF16),
            pltpu.VMEM((PARTS, 2, 2, RIM, GW), BF16),
            pltpu.VMEM((128, 128), F32),
            pltpu.VMEM((WINDOW, HEADS, WINDOW), F32),
            dma((PARTS, 16)),
            dma((PARTS, 16)),
            dma((5,)),
        ],
        name="neighbourhood",
        compiler_params=pltpu.CompilerParams(
            collective_id=0, has_side_effects=True, vmem_limit_bytes=40 * 1024 * 1024),
    )(*args)
    return pl.pallas_call(
        hand_on,
        out_shape=(block, block, block),
        in_specs=[vmem] * 3,
        out_specs=(pl.BlockSpec(memory_space=pltpu.HBM),) * 3,
        scratch_shapes=[dma((3,))],
        name="hand_on",
        compiler_params=pltpu.CompilerParams(vmem_limit_bytes=8 * 1024 * 1024),
    )(*grads)


def solution(mesh):
    spec = P("lat", "lon", None)
    return jax.shard_map(
        functools.partial(on_device, mesh.shape["lat"], mesh.shape["lon"]),
        mesh=mesh,
        in_specs=(spec, spec, spec, spec, P()),
        out_specs=(spec, spec, spec),
        check_vma=False,
    )
```
